32 devices in a mesh: head: 4 (over y, x), blk: 8 (over z, core).
Axes of the slice: x: 2, y: 2, z: 4, core: 2. Of those that a mesh axis runs over, the one named last changes fastest.
Arguments:
- queries: bfloat16 [4096, 2048], P(('blk', 'head')), may hold values from -8 to 8
- keys: bfloat16 [4096, 2048], P(('blk', 'head')), may hold values from -8 to 8
- values: bfloat16 [4096, 2048], P(('blk', 'head')), may hold values from -6 to 6
- grad_out: bfloat16 [4096, 2048], P(('blk', 'head')), may hold values from -6 to 6
- stride_owner: int32 [32, 3], replicated, may hold values from 0 to 7, all different within a row; in each aligned block of 4 rows (0 to 3, 4 to 7, ...) at most 2 rows name the same one
Outputs:
- attended: bfloat16 [4096, 2048], P('blk', 'head')
- grad_queries: bfloat16 [4096, 2048], P('blk', 'head')
- grad_keys: bfloat16 [4096, 2048], P('blk', 'head')
- grad_values: bfloat16 [4096, 2048], P('blk', 'head')
The draws below stay inside these ranges and needn't reach their ends.
Inputs may be any that keep to these rules, and one draw needn't show every extreme that they name: `stride_owner`: each row names 3 different runs. Within each aligned block of 4 rows no run is named by more than 2 rows, a bound that some block reaches.
All inputs are finite; a program needn't handle non-finite values.
Results may differ from the reference program's by a relative error of at most 0.02.
Values may be sent and summed in bfloat16 or wider, within the bound.
A program may use at most 128 MiB of HBM per device.

```python
import math
from functools import partial
import jax
import jax.numpy as jnp
import numpy as np
from jax import lax

HEADS = 16
HEAD_DIM = 128
BLOCK = 128
PICKS = 3
STRIDE = 4
QBLOCKS = 32
TOKENS = 4096
CAP = 2
N_BLK = 8


def draw_queries(key, part):
    drawn = jax.random.normal(jax.random.fold_in(key, 1), (TOKENS, HEADS, HEAD_DIM), jnp.float32)
    drawn = jnp.clip(drawn, -6.0, 6.0)
    return drawn.reshape(TOKENS, HEADS * HEAD_DIM).astype(jnp.bfloat16)


def draw_keys(key, part):
    drawn = jax.random.normal(jax.random.fold_in(key, 3), (TOKENS, HEADS, HEAD_DIM), jnp.float32)
    drawn = jnp.clip(drawn, -6.0, 6.0)
    return drawn.reshape(TOKENS, HEADS * HEAD_DIM).astype(jnp.bfloat16)


def block_levels(rng, dims, pieces, low, largest):
    gain = 1.0
    for axis_at, blocks in pieces:
        heights = jax.random.uniform(jax.random.fold_in(jax.random.fold_in(rng, 6), axis_at), (blocks,), jnp.float32, low / len(pieces), largest / len(pieces))
        gain = gain * jnp.repeat(jnp.exp(heights), dims[axis_at] // blocks).reshape((-1,) + (1,) * (len(dims) - 1 - axis_at))
    return gain


def shared_out(stream_key, own, number, rows, count, top, most, skew):
    order = jax.random.permutation(stream_key, count)
    heavy_load, usual = load_shares(count, rows * top, most, skew, True), load_shares(count, rows * top, most, skew, False)
    places = jnp.arange(count)

    def named(sizes, offset_by):
        used = int((sizes > 0).sum())
        fixed = max(1, used // 4)
        moved = fixed + (places - fixed + offset_by * (used - fixed)) % max(1, count - fixed)
        return jnp.zeros((count,), jnp.int32).at[order[jnp.where(places < fixed, places, moved)]].set(jnp.asarray(sizes, jnp.int32))

    sizes = jnp.where(number % 4 == 0, named(heavy_load, number // 4), named(usual, number - number // 4 - 1))
    mixed = jax.random.permutation(jax.random.fold_in(own, 3), count)
    donor, sink = mixed[0:count // 2 * 2:2], mixed[1:count // 2 * 2:2]
    room = jnp.minimum(sizes[donor] - 1, most - sizes[sink]) // 2
    room = jnp.where((donor == order[0]) | (sink == order[0]) | (sizes[sink] == 0), 0, jnp.maximum(room, 0))
    moved = jax.random.randint(jax.random.fold_in(own, 4), (count // 2,), 0, 1 << 20) % (room + 1)
    sizes = sizes.at[donor].add(-moved).at[sink].add(moved)
    labels = jnp.searchsorted(jnp.cumsum(sizes), jnp.arange(rows * top), side="right").astype(jnp.int32)
    listing = labels.reshape(top, rows).T
    listing = listing[jax.random.permutation(jax.random.fold_in(own, 1), rows)]
    offset_by = jax.random.randint(jax.random.fold_in(own, 2), (rows, 1), 0, top)
    return jnp.take_along_axis(listing, (jnp.arange(top)[None, :] + offset_by) % top, axis=1)


def load_shares(number_of, total, limit, skew, full):
    portions = [(1 << 20) // math.isqrt(rank ** skew) + 1 for rank in range(1, number_of + 1)]
    largest = limit if full else min(limit, max(-(-total // number_of), total * portions[0] // sum(portions)))
    least = 1 if total - largest >= number_of - 1 else 0
    holding, rest = [largest] + [least] * (number_of - 1), total - largest - least * (number_of - 1)
    while rest > 0:
        candidates = [i for i in range(1, number_of) if holding[i] < largest] or [i for i in range(1, number_of) if holding[i] < limit]
        whole, remaining = sum([portions[i] for i in candidates]), rest
        for i in candidates:
            addition = min(limit - holding[i], max(1, remaining * portions[i] // whole), rest)
            holding[i] = holding[i] + addition
            rest = rest - addition
    return np.array(holding)


def noise(stream_key, shape, deviation, most, pieces=(), kind=jnp.bfloat16):
    array = jax.random.normal(stream_key, shape, jnp.float32) * deviation
    if len(pieces) > 0:
        array = block_levels(stream_key, shape, pieces, -0.22, 0.18) * array
    return jnp.clip(array, min=-most, max=most).astype(kind)


def setup_inputs(seed: int = 0) -> dict:
    streams_of = jax.random.split(jax.random.key(seed), 6)
    queries = draw_queries(jax.random.fold_in(streams_of[5], 71), 0)
    keys = draw_keys(jax.random.fold_in(streams_of[5], 71), 0)
    values = noise(streams_of[2], (TOKENS, HEADS * HEAD_DIM), 1.0, 6.0, ((0, 32),))
    grad_out = noise(streams_of[3], (TOKENS, HEADS * HEAD_DIM), 1.0, 6.0, ((0, 32),))
    stride_owner_keys = jax.random.split(jax.random.fold_in(streams_of[4], 1), QBLOCKS // STRIDE)
    stride_owner_turns = jax.random.permutation(jax.random.fold_in(streams_of[4], 3), QBLOCKS // STRIDE)
    stride_owner = jax.vmap(lambda own, number: shared_out(jax.random.fold_in(streams_of[4], 2), own, number, STRIDE, N_BLK, PICKS, CAP, 2))(stride_owner_keys, stride_owner_turns).reshape((QBLOCKS, PICKS))
    return dict(queries=queries, keys=keys, values=values, grad_out=grad_out, stride_owner=stride_owner)


def to_bf16_wide(source):
    return lax.optimization_barrier(source.astype(jnp.bfloat16)).astype(jnp.float32)


def key_table(stride_owner):
    blocks = jnp.arange(QBLOCKS, dtype=jnp.int32)
    offset = (blocks % STRIDE).astype(jnp.int32)
    strided = (stride_owner.astype(jnp.int32) * STRIDE + offset[:, None]).astype(jnp.int32)
    nearby = jnp.stack([(blocks - 1) % QBLOCKS, blocks, (blocks + 1) % QBLOCKS], axis=1).astype(jnp.int32)
    leading = jnp.zeros((QBLOCKS, 2), jnp.int32) + jnp.arange(2, dtype=jnp.int32)[None, :]
    return jnp.concatenate([nearby, strided, leading], axis=1).astype(jnp.int32)


def settle(terms):
    rounded = to_bf16_wide(terms[:, 3:6])
    return jnp.concatenate([terms[:, :3], rounded, terms[:, 6:]], axis=1)


def head_pass(table, operands):
    query_head, key_head, value_head, grad_head = operands
    factor = HEAD_DIM ** -0.5
    key_sets = key_head[table].astype(jnp.float32)
    value_sets = value_head[table].astype(jnp.float32)
    query_wide = query_head.astype(jnp.float32)
    grad_wide = grad_head.astype(jnp.float32)
    scores = jnp.einsum('iqd,ijkd->iqjk', query_wide, key_sets) * factor
    row_max = jnp.max(scores, axis=(2, 3), keepdims=True)
    log_total = row_max + jnp.log(jnp.sum(jnp.exp(scores - row_max), axis=(2, 3), keepdims=True))
    weights = jnp.exp(scores - log_total)
    rounded = to_bf16_wide(weights)
    attended = jnp.einsum('iqjk,ijkd->iqd', rounded, value_sets).astype(jnp.bfloat16)
    grad_weights = jnp.einsum('iqd,ijkd->iqjk', grad_wide, value_sets)
    delta = jnp.sum(grad_wide * attended.astype(jnp.float32), axis=-1)[:, :, None, None]
    grad_scores = to_bf16_wide(weights * (grad_weights - delta) * factor)
    grad_queries = jnp.einsum('iqjk,ijkd->iqd', grad_scores, key_sets).astype(jnp.bfloat16)
    key_terms = settle(jnp.einsum('iqjk,iqd->ijkd', grad_scores, query_wide))
    value_terms = settle(jnp.einsum('iqjk,iqd->ijkd', rounded, grad_wide))
    blank = jnp.zeros((QBLOCKS, BLOCK, HEAD_DIM), jnp.float32)
    grad_keys = blank.at[table].add(key_terms).astype(jnp.bfloat16)
    grad_values = blank.at[table].add(value_terms).astype(jnp.bfloat16)
    return attended, grad_queries, grad_keys, grad_values


def per_head(source):
    return source.reshape(QBLOCKS, BLOCK, HEADS, HEAD_DIM).transpose(2, 0, 1, 3)


def back_rows(source):
    return source.transpose(1, 2, 0, 3).reshape(TOKENS, HEADS * HEAD_DIM)


def reference(queries, keys, values, grad_out, stride_owner):
    table = key_table(stride_owner)
    results = lax.map(partial(head_pass, table), (per_head(queries), per_head(keys), per_head(values), per_head(grad_out)))
    return back_rows(results[0]), back_rows(results[1]), back_rows(results[2]), back_rows(results[3])
```

```python
import math
from functools import partial

import jax
import jax.numpy as jnp
from jax import lax
from jax.experimental import pallas as pl
from jax.experimental.pallas import tpu as pltpu
from jax.sharding import PartitionSpec as P

HEAD_DIM = 128
BLOCK = 128
PICKS = 3
MESH = pl.DeviceIdType.MESH


def with_halo(block, sides, width):
    for axis, dim in sides:
        count = lax.axis_size(axis)
        forward = [(i, i + 1) for i in range(count - 1)]
        forward.append((count - 1, 0))
        backward = [(target, source) for source, target in forward]
        low = lax.ppermute(
            lax.slice_in_dim(block, block.shape[dim] - width, None, axis=dim), axis, forward
        )
        high = lax.ppermute(lax.slice_in_dim(block, 0, width, axis=dim), axis, backward)
        block = jnp.concatenate([low, block, high], axis=dim)
    return block


def from_root(block, axis, holder):
    block = jnp.where(lax.axis_index(axis) == holder, block, jnp.zeros_like(block))
    return lax.psum(block, axis)


def slot_tables(stride_owner, n_blk, blocks, capacity, device):
    owner_table = stride_owner.reshape(n_blk, blocks, PICKS)
    owner_ids = jnp.arange(n_blk, dtype=jnp.int32)
    naming = jnp.any(owner_table[:, :, :, None] == owner_ids[None, None, None, :], axis=2)
    counts = naming.astype(jnp.int32)
    ranking = jnp.cumsum(counts, axis=1) - counts
    naming_here = lax.dynamic_index_in_dim(naming, device, 2, keepdims=False)
    ranking_here = lax.dynamic_index_in_dim(ranking, device, 2, keepdims=False)
    slot_ids = jnp.arange(capacity, dtype=jnp.int32)
    matched = naming_here[:, None, :] & (ranking_here[:, None, :] == slot_ids[None, :, None])
    offsets = jnp.sum(
        matched.astype(jnp.int32) * jnp.arange(blocks, dtype=jnp.int32)[None, None, :], axis=2
    )
    own_rows = lax.dynamic_index_in_dim(owner_table, device, 0, keepdims=False)
    own_ranks = lax.dynamic_index_in_dim(ranking, device, 0, keepdims=False)
    picked = jnp.take_along_axis(own_ranks, own_rows, axis=1)
    flat_slot = own_rows * capacity + picked
    return (offsets.reshape(-1), flat_slot, matched.reshape(n_blk * capacity, blocks))


def fetch_keys(stacked, offsets, flat_slot, capacity):
    seq_rows = stacked.shape[1]
    width = stacked.shape[2]
    blocks = seq_rows // BLOCK
    n_blk = lax.axis_size("blk")
    extended = with_halo(stacked, (("blk", 1),), BLOCK)
    extended = extended.reshape(2, blocks + 2, BLOCK, width)
    block_view = stacked.reshape(2, blocks, BLOCK, width)
    leading = from_root(block_view[:, 0:2], "blk", 0)
    outgoing = jnp.take(block_view, offsets, axis=1).reshape(2, n_blk, capacity, BLOCK, width)
    incoming = lax.all_to_all(outgoing, "blk", split_axis=1, concat_axis=1, tiled=True)
    incoming = incoming.reshape(2, n_blk * capacity, BLOCK, width)
    pooled = jnp.concatenate([extended, incoming, leading], axis=1)
    rows_here = jnp.arange(blocks, dtype=jnp.int32)[:, None]
    nearby_index = rows_here + jnp.arange(3, dtype=jnp.int32)[None, :]
    distant_index = blocks + 2 + flat_slot
    leading_index = (
        jnp.zeros((blocks, 2), jnp.int32)
        + (blocks + 2 + n_blk * capacity)
        + jnp.arange(2, dtype=jnp.int32)[None, :]
    )
    table = jnp.concatenate([nearby_index, distant_index, leading_index], axis=1)
    return jnp.take(pooled, table.reshape(-1), axis=1)


def score_block(query_part, key_part, factor):
    return (
        jnp.einsum("gqhd,gjkhd->ghqjk", query_part, key_part, preferred_element_type=jnp.float32)
        * factor
    )


def log_normal(scores):
    row_max = jnp.max(scores, axis=(3, 4), keepdims=True)
    return row_max + jnp.log(jnp.sum(jnp.exp(scores - row_max), axis=(3, 4), keepdims=True))


def output_of(rounded, value_part):
    return jnp.einsum(
        "ghqjk,gjkhd->gqhd", rounded, value_part, preferred_element_type=jnp.float32
    ).astype(jnp.bfloat16)


def split_terms(coeffs, source):
    group_size = source.shape[0]
    near = jnp.einsum(
        "ghqjk,gqhd->gjkhd", coeffs[:, :, :, 0:3], source, preferred_element_type=jnp.float32
    )
    far = jnp.einsum(
        "ghqjk,gqhd->gjkhd", coeffs[:, :, :, 3:6], source, preferred_element_type=jnp.float32
    ).astype(jnp.bfloat16)
    lead = jnp.einsum(
        "ghqjk,gqhd->jkhd", coeffs[:, :, :, 6:8], source, preferred_element_type=jnp.float32
    )
    near = near.reshape(group_size, 3, near.shape[2], near.shape[3] * near.shape[4])
    far = far.reshape(group_size, 3, far.shape[2], far.shape[3] * far.shape[4])
    lead = lead.reshape(2, lead.shape[1], lead.shape[2] * lead.shape[3])
    return (near, far, lead)


def backward_from(
    scores, log_total, rounded, attended, grad_part, query_part, key_part, value_part, factor
):
    grad_weights = jnp.einsum(
        "gqhd,gjkhd->ghqjk", grad_part, value_part, preferred_element_type=jnp.float32
    )
    delta = jnp.sum(grad_part.astype(jnp.float32) * attended.astype(jnp.float32), axis=3)
    delta = jnp.transpose(delta, (0, 2, 1))[:, :, :, None, None]
    grad_scores = (jnp.exp(scores - log_total) * (grad_weights - delta) * factor).astype(
        jnp.bfloat16
    )
    grad_query = jnp.einsum(
        "ghqjk,gjkhd->gqhd", grad_scores, key_part, preferred_element_type=jnp.float32
    ).astype(jnp.bfloat16)
    key_near, key_far, key_lead = split_terms(grad_scores, query_part)
    value_near, value_far, value_lead = split_terms(rounded, grad_part)
    return (grad_query, key_near, key_far, key_lead, value_near, value_far, value_lead)


def spread_near(near_terms, width):
    blank = jnp.zeros((1, BLOCK, width), jnp.float32)
    return (
        jnp.concatenate([near_terms[:, 0], blank, blank], axis=0)
        + jnp.concatenate([blank, near_terms[:, 1], blank], axis=0)
        + jnp.concatenate([blank, blank, near_terms[:, 2]], axis=0)
    )


def by_runs(queries, keys, values, grad_out, stride_owner):
    query_rows, key_rows, value_rows, grad_rows = (
        lax.all_to_all(queries, "head", split_axis=1, concat_axis=0, tiled=True),
        lax.all_to_all(keys, "head", split_axis=1, concat_axis=0, tiled=True),
        lax.all_to_all(values, "head", split_axis=1, concat_axis=0, tiled=True),
        lax.all_to_all(grad_out, "head", split_axis=1, concat_axis=0, tiled=True),
    )
    seq_rows, width = query_rows.shape
    heads_here = width // HEAD_DIM
    blocks = seq_rows // BLOCK
    n_blk = lax.axis_size("blk")
    capacity = max(2, (PICKS * blocks + n_blk - 1) // n_blk)
    device = lax.axis_index("blk")
    offsets, flat_slot, matched = slot_tables(stride_owner, n_blk, blocks, capacity, device)
    group_size = math.gcd(blocks, max(1, 512 // BLOCK))
    group_count = blocks // group_size
    factor = HEAD_DIM ** (-0.5)
    stacked = jnp.stack([key_rows, value_rows])
    query_view = query_rows.reshape(blocks, BLOCK, heads_here, HEAD_DIM)
    grad_view = grad_rows.reshape(blocks, BLOCK, heads_here, HEAD_DIM)
    key_sets = fetch_keys(stacked, offsets, flat_slot, capacity)
    key_sets = key_sets.reshape(2, blocks, 8, BLOCK, heads_here, HEAD_DIM)

    def pieces(group_id):
        start = group_id * group_size
        query_part = lax.dynamic_slice_in_dim(query_view, start, group_size, 0)
        grad_part = lax.dynamic_slice_in_dim(grad_view, start, group_size, 0)
        kv_part = lax.dynamic_slice_in_dim(key_sets, start, group_size, 1)
        return (query_part, grad_part, kv_part[0], kv_part[1])

    def joined_pass(group_id):
        query_part, grad_part, key_part, value_part = pieces(group_id)
        scores = score_block(query_part, key_part, factor)
        log_total = log_normal(scores)
        rounded = jnp.exp(scores - log_total).astype(jnp.bfloat16)
        attended = output_of(rounded, value_part)
        extra = backward_from(
            scores,
            log_total,
            rounded,
            attended,
            grad_part,
            query_part,
            key_part,
            value_part,
            factor,
        )
        return (attended,) + extra

    group_ids = jnp.arange(group_count, dtype=jnp.int32)
    results = lax.map(joined_pass, group_ids)
    attended = results[0]
    grad_query, key_near, key_far, key_lead, value_near, value_far, value_lead = results[1:]
    key_ext = spread_near(key_near.reshape(blocks, 3, BLOCK, width), width)
    value_ext = spread_near(value_near.reshape(blocks, 3, BLOCK, width), width)
    rim_terms = jnp.stack(
        [
            jnp.stack([key_ext[0], value_ext[0]]),
            jnp.stack([key_ext[blocks + 1], value_ext[blocks + 1]]),
        ]
    )
    beside = with_halo(rim_terms.astype(jnp.bfloat16), (("blk", 0),), 1).astype(rim_terms.dtype)
    key_owned = key_ext[1 : blocks + 1].at[0].add(beside[0, 0]).at[blocks - 1].add(beside[3, 0])
    value_owned = value_ext[1 : blocks + 1].at[0].add(beside[0, 1]).at[blocks - 1].add(beside[3, 1])
    slot_flat = flat_slot.reshape(-1)
    key_back = (
        jnp.zeros((n_blk * capacity, BLOCK, width), jnp.bfloat16)
        .at[slot_flat]
        .set(key_far.reshape(blocks * PICKS, BLOCK, width))
    )
    value_back = (
        jnp.zeros((n_blk * capacity, BLOCK, width), jnp.bfloat16)
        .at[slot_flat]
        .set(value_far.reshape(blocks * PICKS, BLOCK, width))
    )
    key_arrived, value_arrived = (
        lax.all_to_all(
            key_back.reshape(n_blk, capacity, BLOCK, width),
            "blk",
            split_axis=0,
            concat_axis=0,
            tiled=True,
        ),
        lax.all_to_all(
            value_back.reshape(n_blk, capacity, BLOCK, width),
            "blk",
            split_axis=0,
            concat_axis=0,
            tiled=True,
        ),
    )
    match_b = matched.astype(jnp.bfloat16)
    key_owned = key_owned + jnp.einsum(
        "sr,sbc->rbc",
        match_b,
        key_arrived.reshape(n_blk * capacity, BLOCK, width),
        preferred_element_type=jnp.float32,
    )
    value_owned = value_owned + jnp.einsum(
        "sr,sbc->rbc",
        match_b,
        value_arrived.reshape(n_blk * capacity, BLOCK, width),
        preferred_element_type=jnp.float32,
    )
    key_total, value_total = (
        lax.psum(jnp.sum(key_lead, axis=0).astype(jnp.bfloat16), "blk").astype(jnp.float32),
        lax.psum(jnp.sum(value_lead, axis=0).astype(jnp.bfloat16), "blk").astype(jnp.float32),
    )
    at_root = device == 0
    key_owned = key_owned.at[0:2].add(jnp.where(at_root, key_total, jnp.zeros_like(key_total)))
    value_owned = value_owned.at[0:2].add(
        jnp.where(at_root, value_total, jnp.zeros_like(value_total))
    )
    grad_keys = key_owned.astype(jnp.bfloat16).reshape(seq_rows, width)
    grad_values = value_owned.astype(jnp.bfloat16).reshape(seq_rows, width)
    return (
        attended.reshape(seq_rows, width),
        grad_query.reshape(seq_rows, width),
        grad_keys,
        grad_values,
    )


def exchange_barrier(peers):
    barrier = pltpu.get_barrier_semaphore()
    for peer in peers:
        pl.semaphore_signal(barrier, inc=1, device_id=peer, device_id_type=MESH)
    pl.semaphore_wait(barrier, len(peers))


def head_kernel(
    n_head,
    n_z,
    owner_ref,
    q_in,
    k_in,
    v_in,
    g_in,
    o_out,
    dq_out,
    dk_out,
    dv_out,
    q_all,
    k_all,
    v_all,
    g_all,
    k_sum,
    v_sum,
    k_far,
    v_far,
    o_stage,
    dq_stage,
    dk_stage,
    dv_stage,
    k_give,
    v_give,
    k_take,
    v_take,
    in_send,
    in_recv,
    pass_send,
    pass_recv,
    own_sem,
    out_send,
    out_recv,
    out_own,
    pair_send,
    pair_recv,
):
    head = lax.axis_index("head")
    blk = lax.axis_index("blk")
    z = blk // 2
    c = blk % 2
    runs = n_head
    total_blocks = 2 * n_z * runs
    factor = HEAD_DIM ** (-0.5)
    sibling = {"head": head, "blk": 2 * z + 1 - c}
    offsets = [(dz, dh) for dz in range(n_z) for dh in range(n_head)]
    far_first = [dz for dz in (2, 1, 3, 0) if dz < n_z] + list(range(4, n_z))
    near_first = [0] + [dz for dz in far_first if dz != 0][::-1]

    def columns(head_id):
        return pl.ds(pl.multiple_of(head_id * HEAD_DIM, HEAD_DIM), HEAD_DIM)

    def to_peer(dz, dh):
        return (z + dz) % n_z, (head + dh) % n_head

    def from_peer(dz, dh):
        return (z + n_z - dz) % n_z, (head + n_head - dh) % n_head

    peers = []
    for dz, dh in offsets:
        if (dz, dh) != (0, 0):
            z2, h2 = to_peer(dz, dh)
            peers.append({"head": h2, "blk": 2 * z2 + c})
    exchange_barrier(peers + [sibling])

    key_pairs = ((0, k_in, k_all), (1, v_in, v_all))
    row_pairs = ((2, q_in, q_all), (3, g_in, g_all))
    mine = blk * runs + head
    my_row = z * runs + head
    my_head = head * n_z + z

    def push(at, source, target, slot, dz, dh):
        z2, h2 = to_peer(dz, dh)
        return pltpu.make_async_remote_copy(
            src_ref=source.at[:, columns(h2 * n_z + z2)],
            dst_ref=target.at[slot],
            send_sem=in_send.at[at, z2 * n_head + h2],
            recv_sem=in_recv.at[at, my_row],
            device_id={"head": h2, "blk": 2 * z2 + c},
            device_id_type=MESH,
        )

    def arrival(at, source, target, slot, dz, dh):
        z1, h1 = from_peer(dz, dh)
        return pltpu.make_async_remote_copy(
            src_ref=source.at[:, columns(my_head)],
            dst_ref=target.at[slot],
            send_sem=in_send.at[at, z1 * n_head + h1],
            recv_sem=in_recv.at[at, z1 * n_head + h1],
            device_id=sibling,
            device_id_type=MESH,
        )

    sends = []
    own_copies = []
    for at, source, target in key_pairs:
        own_copies.append(
            pltpu.make_async_copy(
                source.at[:, columns(my_head)], target.at[mine], own_sem.at[at]
            )
        )
        own_copies[-1].start()
    for dz in far_first:
        for dh in range(n_head):
            if (dz, dh) == (0, 0):
                continue
            for at, source, target in key_pairs:
                copy = push(at, source, target, mine, dz, dh)
                copy.start()
                sends.append(copy)
    passes = []
    for at, source, target in key_pairs:
        copy = pltpu.make_async_remote_copy(
            src_ref=source.at[:, columns(my_head)],
            dst_ref=target.at[mine],
            send_sem=pass_send.at[at, my_row],
            recv_sem=pass_recv.at[at, my_row],
            device_id=sibling,
            device_id_type=MESH,
        )
        copy.start()
        passes.append(copy)
    for at, source, target in row_pairs:
        own_copies.append(
            pltpu.make_async_copy(
                source.at[:, columns(my_head)], target.at[my_row], own_sem.at[at]
            )
        )
        own_copies[-1].start()
    for dz in near_first:
        for dh in range(n_head):
            if (dz, dh) == (0, 0):
                continue
            for at, source, target in row_pairs:
                copy = push(at, source, target, my_row, dz, dh)
                copy.start()
                sends.append(copy)

    blank = jnp.zeros((BLOCK, HEAD_DIM), jnp.float32)

    def clear(n, carry):
        k_sum[n] = blank
        v_sum[n] = blank
        return carry

    lax.fori_loop(0, total_blocks, clear, 0)
    none = n_z * runs * PICKS
    k_far[none] = blank.astype(jnp.bfloat16)
    v_far[none] = blank.astype(jnp.bfloat16)

    for dz in [0] + [d for d in far_first if d != 0]:
        for dh in range(n_head):
            if (dz, dh) == (0, 0):
                continue
            z1, h1 = from_peer(dz, dh)
            block = (2 * z1 + c) * runs + h1
            for at, source, target in key_pairs:
                arrival(at, source, target, block, dz, dh).wait_recv()
                copy = pltpu.make_async_remote_copy(
                    src_ref=target.at[block],
                    dst_ref=target.at[block],
                    send_sem=pass_send.at[at, z1 * n_head + h1],
                    recv_sem=pass_recv.at[at, z1 * n_head + h1],
                    device_id=sibling,
                    device_id_type=MESH,
                )
                copy.start()
                passes.append(copy)
    for copy in own_copies:
        copy.wait()
    for row in range(n_z * n_head):
        z1, h1 = row // n_head, row % n_head
        block = (2 * z1 + 1 - c) * runs + h1
        for at, source, target in key_pairs:
            pltpu.make_async_remote_copy(
                src_ref=target.at[block],
                dst_ref=target.at[block],
                send_sem=pass_send.at[at, row],
                recv_sem=pass_recv.at[at, row],
                device_id=sibling,
                device_id_type=MESH,
            ).wait_recv()

    def contract(left, right, dims):
        return lax.dot_general(
            left, right, ((dims[:1], dims[1:]), ((), ())), preferred_element_type=jnp.float32
        )

    def query_step(z1, r):
        row = z1 * runs + r
        block = (2 * z1 + c) * runs + r
        low = (block + total_blocks - 1) % total_blocks
        high = (block + 1) % total_blocks
        picks = [owner_ref[block, j] * runs + r for j in range(PICKS)]
        named = [low, block, high] + picks + [0, 1]
        keys = jnp.concatenate([k_all[n] for n in named], axis=0)
        values = jnp.concatenate([v_all[n] for n in named], axis=0)
        query = q_all[row]
        grad = g_all[row]
        scores = contract(keys, query, (1, 1))
        top = jnp.max(scores, axis=0, keepdims=True)
        weights = jnp.exp((scores - top) * factor)
        weights = weights * (1.0 / jnp.sum(weights, axis=0, keepdims=True))
        rounded = weights.astype(jnp.bfloat16)
        grad_weights = contract(values, grad, (1, 1))
        delta = jnp.sum(weights * grad_weights, axis=0, keepdims=True)
        grad_scores = (weights * (grad_weights - delta) * factor).astype(jnp.bfloat16)
        o_stage[row] = contract(rounded, values, (0, 0)).astype(jnp.bfloat16)
        dq_stage[row] = contract(grad_scores, keys, (0, 0)).astype(jnp.bfloat16)
        key_terms = contract(grad_scores, query, (1, 0))
        value_terms = contract(rounded, grad, (1, 0))
        for j, n in ((0, low), (1, block), (2, high), (6, 0), (7, 1)):
            k_sum[n] += key_terms[j * BLOCK : (j + 1) * BLOCK]
            v_sum[n] += value_terms[j * BLOCK : (j + 1) * BLOCK]
        for j in range(PICKS):
            rows = slice((3 + j) * BLOCK, (4 + j) * BLOCK)
            k_far[row * PICKS + j] = key_terms[rows].astype(jnp.bfloat16)
            v_far[row * PICKS + j] = value_terms[rows].astype(jnp.bfloat16)

    def hand_out(pairs, dz):
        for at, stage, out in pairs:
            z2 = (z + n_z - dz) % n_z
            for r in range(runs):
                source = stage.at[z2 * runs + r]
                rows = pl.ds(r * BLOCK, BLOCK)
                if dz == 0:
                    copy = pltpu.make_async_copy(
                        source, out.at[rows, columns(z)], out_own.at[at, r]
                    )
                    copy.start()
                    own_outs.append(copy)
                else:
                    copy = pltpu.make_async_remote_copy(
                        src_ref=source,
                        dst_ref=out.at[rows, columns(z)],
                        send_sem=out_send.at[at, z2 * runs + r],
                        recv_sem=out_recv.at[at, z * runs + r],
                        device_id={"head": head, "blk": 2 * z2 + c},
                        device_id_type=MESH,
                    )
                    copy.start()
                    sends.append(copy)

    own_outs = []
    row_outs = ((0, o_stage, o_out), (1, dq_stage, dq_out))
    key_outs = ((2, dk_stage, dk_out), (3, dv_stage, dv_out))
    for dz in near_first:
        z1 = (z + n_z - dz) % n_z
        for dh in range(n_head):
            if (dz, dh) == (0, 0):
                continue
            h1 = (head + n_head - dh) % n_head
            for at, source, target in row_pairs:
                arrival(at, source, target, z1 * runs + h1, dz, dh).wait_recv()

        def step(r, carry, z1=z1):
            query_step(z1, r)
            return carry

        lax.fori_loop(0, runs, step, 0)
        hand_out(row_outs, dz)

    def total_of(sums, far, run, r):
        total = sums[run * runs + r]
        for z1 in range(n_z):
            block = (2 * z1 + c) * runs + r
            row = z1 * runs + r
            place = none
            for j in range(PICKS):
                place = jnp.where(owner_ref[block, j] == run, row * PICKS + j, place)
            total = total + far[place].astype(jnp.float32)
        return total

    def give_step(row, carry):
        run, r = 2 * (row // runs) + 1 - c, row % runs
        k_give[row] = total_of(k_sum, k_far, run, r).astype(jnp.bfloat16)
        v_give[row] = total_of(v_sum, v_far, run, r).astype(jnp.bfloat16)
        return carry

    lax.fori_loop(0, n_z * runs, give_step, 0)
    pair_copies = []
    for at, give, take in ((0, k_give, k_take), (1, v_give, v_take)):
        copy = pltpu.make_async_remote_copy(
            src_ref=give,
            dst_ref=take,
            send_sem=pair_send.at[at],
            recv_sem=pair_recv.at[at],
            device_id=sibling,
            device_id_type=MESH,
        )
        copy.start()
        pair_copies.append(copy)
    for copy in pair_copies:
        copy.wait_recv()
    for dz in far_first:
        z1 = (z + n_z - dz) % n_z

        def join_step(r, carry, z1=z1):
            row, run = z1 * runs + r, 2 * z1 + c
            for sums, far, take, stage in (
                (k_sum, k_far, k_take, dk_stage),
                (v_sum, v_far, v_take, dv_stage),
            ):
                total = total_of(sums, far, run, r) + take[row].astype(jnp.float32)
                stage[row] = total.astype(jnp.bfloat16)
            return carry

        lax.fori_loop(0, runs, join_step, 0)
        hand_out(key_outs, dz)

    for dz in range(1, n_z):
        z1 = (z + n_z - dz) % n_z
        for at, stage, out in row_outs + key_outs:
            for r in range(runs):
                pltpu.make_async_remote_copy(
                    src_ref=stage.at[z1 * runs + r],
                    dst_ref=out.at[pl.ds(r * BLOCK, BLOCK), columns(z1)],
                    send_sem=out_send.at[at, z1 * runs + r],
                    recv_sem=out_recv.at[at, z1 * runs + r],
                    device_id=sibling,
                    device_id_type=MESH,
                ).wait_recv()
    for copy in own_outs:
        copy.wait()
    for copy in sends + passes + pair_copies:
        copy.wait_send()


def by_heads(queries, keys, values, grad_out, stride_owner):
    n_head, n_blk = lax.axis_size("head"), lax.axis_size("blk")
    n_z = n_blk // 2
    rows = n_z * n_head
    seq_rows, width = BLOCK * n_head, n_z * HEAD_DIM
    tile = (BLOCK, HEAD_DIM)
    low, wide = jnp.bfloat16, jnp.float32
    dma = pltpu.SemaphoreType.DMA
    out = jax.ShapeDtypeStruct((seq_rows, width), low)
    anywhere = pl.BlockSpec(memory_space=pl.ANY)
    return pl.pallas_call(
        partial(head_kernel, n_head, n_z),
        out_shape=(out,) * 4,
        in_specs=[pl.BlockSpec(memory_space=pltpu.SMEM)] + [anywhere] * 4,
        out_specs=(anywhere,) * 4,
        scratch_shapes=[
            pltpu.VMEM((rows,) + tile, low),
            pltpu.VMEM((2 * rows,) + tile, low),
            pltpu.VMEM((2 * rows,) + tile, low),
            pltpu.VMEM((rows,) + tile, low),
            pltpu.VMEM((2 * rows,) + tile, wide),
            pltpu.VMEM((2 * rows,) + tile, wide),
            pltpu.VMEM((rows * PICKS + 1,) + tile, low),
            pltpu.VMEM((rows * PICKS + 1,) + tile, low),
        ]
        + [pltpu.VMEM((rows,) + tile, low)] * 8
        + [
            dma((4, rows)),
            dma((4, rows)),
            dma((2, rows)),
            dma((2, rows)),
            dma((4,)),
            dma((4, rows)),
            dma((4, rows)),
            dma((4, n_head)),
            dma((2,)),
            dma((2,)),
        ],
        compiler_params=pltpu.CompilerParams(
            collective_id=0, has_side_effects=True, vmem_limit_bytes=48 * 1024 * 1024
        ),
    )(stride_owner, queries, keys, values, grad_out)


def on_device(queries, keys, values, grad_out, stride_owner):
    n_head, n_blk = lax.axis_size("head"), lax.axis_size("blk")
    rows, width = queries.shape
    if rows == BLOCK and n_blk % 2 == 0 and width == n_head * (n_blk // 2) * HEAD_DIM:
        return by_heads(queries, keys, values, grad_out, stride_owner)
    return by_runs(queries, keys, values, grad_out, stride_owner)


def solution(mesh):
    return jax.shard_map(
        on_device,
        mesh=mesh,
        in_specs=(
            P(("blk", "head"), None),
            P(("blk", "head"), None),
            P(("blk", "head"), None),
            P(("blk", "head"), None),
            P(),
        ),
        out_specs=(P("blk", "head"), P("blk", "head"), P("blk", "head"), P("blk", "head")),
        check_vma=False,
    )
```

```python
import math
from functools import partial

import jax
import jax.numpy as jnp
from jax import lax
from jax.experimental import pallas as pl
from jax.experimental.pallas import tpu as pltpu
from jax.sharding import PartitionSpec as P

HEAD_DIM = 128
BLOCK = 128
PICKS = 3
MESH = pl.DeviceIdType.MESH


def with_halo(block, sides, width):
    for axis, dim in sides:
        count = lax.axis_size(axis)
        forward = [(i, i + 1) for i in range(count - 1)]
        forward.append((count - 1, 0))
        backward = [(target, source) for source, target in forward]
        low = lax.ppermute(
            lax.slice_in_dim(block, block.shape[dim] - width, None, axis=dim), axis, forward
        )
        high = lax.ppermute(lax.slice_in_dim(block, 0, width, axis=dim), axis, backward)
        block = jnp.concatenate([low, block, high], axis=dim)
    return block


def from_root(block, axis, holder):
    block = jnp.where(lax.axis_index(axis) == holder, block, jnp.zeros_like(block))
    return lax.psum(block, axis)


def slot_tables(stride_owner, n_blk, blocks, capacity, device):
    owner_table = stride_owner.reshape(n_blk, blocks, PICKS)
    owner_ids = jnp.arange(n_blk, dtype=jnp.int32)
    naming = jnp.any(owner_table[:, :, :, None] == owner_ids[None, None, None, :], axis=2)
    counts = naming.astype(jnp.int32)
    ranking = jnp.cumsum(counts, axis=1) - counts
    naming_here = lax.dynamic_index_in_dim(naming, device, 2, keepdims=False)
    ranking_here = lax.dynamic_index_in_dim(ranking, device, 2, keepdims=False)
    slot_ids = jnp.arange(capacity, dtype=jnp.int32)
    matched = naming_here[:, None, :] & (ranking_here[:, None, :] == slot_ids[None, :, None])
    offsets = jnp.sum(
        matched.astype(jnp.int32) * jnp.arange(blocks, dtype=jnp.int32)[None, None, :], axis=2
    )
    own_rows = lax.dynamic_index_in_dim(owner_table, device, 0, keepdims=False)
    own_ranks = lax.dynamic_index_in_dim(ranking, device, 0, keepdims=False)
    picked = jnp.take_along_axis(own_ranks, own_rows, axis=1)
    flat_slot = own_rows * capacity + picked
    return (offsets.reshape(-1), flat_slot, matched.reshape(n_blk * capacity, blocks))


def fetch_keys(stacked, offsets, flat_slot, capacity):
    seq_rows = stacked.shape[1]
    width = stacked.shape[2]
    blocks = seq_rows // BLOCK
    n_blk = lax.axis_size("blk")
    extended = with_halo(stacked, (("blk", 1),), BLOCK)
    extended = extended.reshape(2, blocks + 2, BLOCK, width)
    block_view = stacked.reshape(2, blocks, BLOCK, width)
    leading = from_root(block_view[:, 0:2], "blk", 0)
    outgoing = jnp.take(block_view, offsets, axis=1).reshape(2, n_blk, capacity, BLOCK, width)
    incoming = lax.all_to_all(outgoing, "blk", split_axis=1, concat_axis=1, tiled=True)
    incoming = incoming.reshape(2, n_blk * capacity, BLOCK, width)
    pooled = jnp.concatenate([extended, incoming, leading], axis=1)
    rows_here = jnp.arange(blocks, dtype=jnp.int32)[:, None]
    nearby_index = rows_here + jnp.arange(3, dtype=jnp.int32)[None, :]
    distant_index = blocks + 2 + flat_slot
    leading_index = (
        jnp.zeros((blocks, 2), jnp.int32)
        + (blocks + 2 + n_blk * capacity)
        + jnp.arange(2, dtype=jnp.int32)[None, :]
    )
    table = jnp.concatenate([nearby_index, distant_index, leading_index], axis=1)
    return jnp.take(pooled, table.reshape(-1), axis=1)


def score_block(query_part, key_part, factor):
    return (
        jnp.einsum("gqhd,gjkhd->ghqjk", query_part, key_part, preferred_element_type=jnp.float32)
        * factor
    )


def log_normal(scores):
    row_max = jnp.max(scores, axis=(3, 4), keepdims=True)
    return row_max + jnp.log(jnp.sum(jnp.exp(scores - row_max), axis=(3, 4), keepdims=True))


def output_of(rounded, value_part):
    return jnp.einsum(
        "ghqjk,gjkhd->gqhd", rounded, value_part, preferred_element_type=jnp.float32
    ).astype(jnp.bfloat16)


def split_terms(coeffs, source):
    group_size = source.shape[0]
    near = jnp.einsum(
        "ghqjk,gqhd->gjkhd", coeffs[:, :, :, 0:3], source, preferred_element_type=jnp.float32
    )
    far = jnp.einsum(
        "ghqjk,gqhd->gjkhd", coeffs[:, :, :, 3:6], source, preferred_element_type=jnp.float32
    ).astype(jnp.bfloat16)
    lead = jnp.einsum(
        "ghqjk,gqhd->jkhd", coeffs[:, :, :, 6:8], source, preferred_element_type=jnp.float32
    )
    near = near.reshape(group_size, 3, near.shape[2], near.shape[3] * near.shape[4])
    far = far.reshape(group_size, 3, far.shape[2], far.shape[3] * far.shape[4])
    lead = lead.reshape(2, lead.shape[1], lead.shape[2] * lead.shape[3])
    return (near, far, lead)


def backward_from(
    scores, log_total, rounded, attended, grad_part, query_part, key_part, value_part, factor
):
    grad_weights = jnp.einsum(
        "gqhd,gjkhd->ghqjk", grad_part, value_part, preferred_element_type=jnp.float32
    )
    delta = jnp.sum(grad_part.astype(jnp.float32) * attended.astype(jnp.float32), axis=3)
    delta = jnp.transpose(delta, (0, 2, 1))[:, :, :, None, None]
    grad_scores = (jnp.exp(scores - log_total) * (grad_weights - delta) * factor).astype(
        jnp.bfloat16
    )
    grad_query = jnp.einsum(
        "ghqjk,gjkhd->gqhd", grad_scores, key_part, preferred_element_type=jnp.float32
    ).astype(jnp.bfloat16)
    key_near, key_far, key_lead = split_terms(grad_scores, query_part)
    value_near, value_far, value_lead = split_terms(rounded, grad_part)
    return (grad_query, key_near, key_far, key_lead, value_near, value_far, value_lead)


def spread_near(near_terms, width):
    blank = jnp.zeros((1, BLOCK, width), jnp.float32)
    return (
        jnp.concatenate([near_terms[:, 0], blank, blank], axis=0)
        + jnp.concatenate([blank, near_terms[:, 1], blank], axis=0)
        + jnp.concatenate([blank, blank, near_terms[:, 2]], axis=0)
    )


def by_runs(queries, keys, values, grad_out, stride_owner):
    query_rows, key_rows, value_rows, grad_rows = (
        lax.all_to_all(queries, "head", split_axis=1, concat_axis=0, tiled=True),
        lax.all_to_all(keys, "head", split_axis=1, concat_axis=0, tiled=True),
        lax.all_to_all(values, "head", split_axis=1, concat_axis=0, tiled=True),
        lax.all_to_all(grad_out, "head", split_axis=1, concat_axis=0, tiled=True),
    )
    seq_rows, width = query_rows.shape
    heads_here = width // HEAD_DIM
    blocks = seq_rows // BLOCK
    n_blk = lax.axis_size("blk")
    capacity = max(2, (PICKS * blocks + n_blk - 1) // n_blk)
    device = lax.axis_index("blk")
    offsets, flat_slot, matched = slot_tables(stride_owner, n_blk, blocks, capacity, device)
    group_size = math.gcd(blocks, max(1, 512 // BLOCK))
    group_count = blocks // group_size
    factor = HEAD_DIM ** (-0.5)
    stacked = jnp.stack([key_rows, value_rows])
    query_view = query_rows.reshape(blocks, BLOCK, heads_here, HEAD_DIM)
    grad_view = grad_rows.reshape(blocks, BLOCK, heads_here, HEAD_DIM)
    key_sets = fetch_keys(stacked, offsets, flat_slot, capacity)
    key_sets = key_sets.reshape(2, blocks, 8, BLOCK, heads_here, HEAD_DIM)

    def pieces(group_id):
        start = group_id * group_size
        query_part = lax.dynamic_slice_in_dim(query_view, start, group_size, 0)
        grad_part = lax.dynamic_slice_in_dim(grad_view, start, group_size, 0)
        kv_part = lax.dynamic_slice_in_dim(key_sets, start, group_size, 1)
        return (query_part, grad_part, kv_part[0], kv_part[1])

    def joined_pass(group_id):
        query_part, grad_part, key_part, value_part = pieces(group_id)
        scores = score_block(query_part, key_part, factor)
        log_total = log_normal(scores)
        rounded = jnp.exp(scores - log_total).astype(jnp.bfloat16)
        attended = output_of(rounded, value_part)
        extra = backward_from(
            scores,
            log_total,
            rounded,
            attended,
            grad_part,
            query_part,
            key_part,
            value_part,
            factor,
        )
        return (attended,) + extra

    group_ids = jnp.arange(group_count, dtype=jnp.int32)
    results = lax.map(joined_pass, group_ids)
    attended = results[0]
    grad_query, key_near, key_far, key_lead, value_near, value_far, value_lead = results[1:]
    key_ext = spread_near(key_near.reshape(blocks, 3, BLOCK, width), width)
    value_ext = spread_near(value_near.reshape(blocks, 3, BLOCK, width), width)
    rim_terms = jnp.stack(
        [
            jnp.stack([key_ext[0], value_ext[0]]),
            jnp.stack([key_ext[blocks + 1], value_ext[blocks + 1]]),
        ]
    )
    beside = with_halo(rim_terms.astype(jnp.bfloat16), (("blk", 0),), 1).astype(rim_terms.dtype)
    key_owned = key_ext[1 : blocks + 1].at[0].add(beside[0, 0]).at[blocks - 1].add(beside[3, 0])
    value_owned = value_ext[1 : blocks + 1].at[0].add(beside[0, 1]).at[blocks - 1].add(beside[3, 1])
    slot_flat = flat_slot.reshape(-1)
    key_back = (
        jnp.zeros((n_blk * capacity, BLOCK, width), jnp.bfloat16)
        .at[slot_flat]
        .set(key_far.reshape(blocks * PICKS, BLOCK, width))
    )
    value_back = (
        jnp.zeros((n_blk * capacity, BLOCK, width), jnp.bfloat16)
        .at[slot_flat]
        .set(value_far.reshape(blocks * PICKS, BLOCK, width))
    )
    key_arrived, value_arrived = (
        lax.all_to_all(
            key_back.reshape(n_blk, capacity, BLOCK, width),
            "blk",
            split_axis=0,
            concat_axis=0,
            tiled=True,
        ),
        lax.all_to_all(
            value_back.reshape(n_blk, capacity, BLOCK, width),
            "blk",
            split_axis=0,
            concat_axis=0,
            tiled=True,
        ),
    )
    match_b = matched.astype(jnp.bfloat16)
    key_owned = key_owned + jnp.einsum(
        "sr,sbc->rbc",
        match_b,
        key_arrived.reshape(n_blk * capacity, BLOCK, width),
        preferred_element_type=jnp.float32,
    )
    value_owned = value_owned + jnp.einsum(
        "sr,sbc->rbc",
        match_b,
        value_arrived.reshape(n_blk * capacity, BLOCK, width),
        preferred_element_type=jnp.float32,
    )
    key_total, value_total = (
        lax.psum(jnp.sum(key_lead, axis=0).astype(jnp.bfloat16), "blk").astype(jnp.float32),
        lax.psum(jnp.sum(value_lead, axis=0).astype(jnp.bfloat16), "blk").astype(jnp.float32),
    )
    at_root = device == 0
    key_owned = key_owned.at[0:2].add(jnp.where(at_root, key_total, jnp.zeros_like(key_total)))
    value_owned = value_owned.at[0:2].add(
        jnp.where(at_root, value_total, jnp.zeros_like(value_total))
    )
    grad_keys = key_owned.astype(jnp.bfloat16).reshape(seq_rows, width)
    grad_values = value_owned.astype(jnp.bfloat16).reshape(seq_rows, width)
    return (
        attended.reshape(seq_rows, width),
        grad_query.reshape(seq_rows, width),
        grad_keys,
        grad_values,
    )


def exchange_barrier(peers):
    barrier = pltpu.get_barrier_semaphore()
    for peer in peers:
        pl.semaphore_signal(barrier, inc=1, device_id=peer, device_id_type=MESH)
    pl.semaphore_wait(barrier, len(peers))


def head_kernel(
    n_head,
    n_z,
    owner_in,
    q_in,
    k_in,
    v_in,
    g_in,
    o_out,
    dq_out,
    dk_out,
    dv_out,
    owner_ref,
    q_all,
    k_all,
    v_all,
    g_all,
    k_sum,
    v_sum,
    k_far,
    v_far,
    o_stage,
    dq_stage,
    dk_stage,
    dv_stage,
    k_give,
    v_give,
    k_take,
    v_take,
    in_send,
    in_recv,
    pass_send,
    pass_recv,
    own_sem,
    out_send,
    out_recv,
    out_own,
    pair_send,
    pair_recv,
):
    head = lax.axis_index("head")
    blk = lax.axis_index("blk")
    z = blk // 2
    c = blk % 2
    runs = n_head
    total_blocks = 2 * n_z * runs
    factor = HEAD_DIM ** (-0.5)
    sibling = {"head": head, "blk": 2 * z + 1 - c}
    offsets = [(dz, dh) for dz in range(n_z) for dh in range(n_head)]
    far_first = [dz for dz in (2, 1, 3, 0) if dz < n_z] + list(range(4, n_z))
    near_first = [0] + [dz for dz in far_first if dz != 0][::-1]

    def columns(head_id):
        return pl.ds(pl.multiple_of(head_id * HEAD_DIM, HEAD_DIM), HEAD_DIM)

    def to_peer(dz, dh):
        return (z + dz) % n_z, (head + dh) % n_head

    def from_peer(dz, dh):
        return (z + n_z - dz) % n_z, (head + n_head - dh) % n_head

    peers = []
    for dz, dh in offsets:
        if (dz, dh) != (0, 0):
            z2, h2 = to_peer(dz, dh)
            peers.append({"head": h2, "blk": 2 * z2 + c})
    exchange_barrier(peers + [sibling])

    key_pairs = ((0, k_in, k_all), (1, v_in, v_all))
    row_pairs = ((2, q_in, q_all), (3, g_in, g_all))
    mine = blk * runs + head
    my_row = z * runs + head
    my_head = head * n_z + z

    def push(at, source, target, slot, dz, dh):
        z2, h2 = to_peer(dz, dh)
        return pltpu.make_async_remote_copy(
            src_ref=source.at[:, columns(h2 * n_z + z2)],
            dst_ref=target.at[slot],
            send_sem=in_send.at[at, z2 * n_head + h2],
            recv_sem=in_recv.at[at, my_row],
            device_id={"head": h2, "blk": 2 * z2 + c},
            device_id_type=MESH,
        )

    def arrival(at, source, target, slot, dz, dh):
        z1, h1 = from_peer(dz, dh)
        return pltpu.make_async_remote_copy(
            src_ref=source.at[:, columns(my_head)],
            dst_ref=target.at[slot],
            send_sem=in_send.at[at, z1 * n_head + h1],
            recv_sem=in_recv.at[at, z1 * n_head + h1],
            device_id=sibling,
            device_id_type=MESH,
        )

    sends = []
    own_copies = [pltpu.make_async_copy(owner_in, owner_ref, own_sem.at[4])]
    own_copies[0].start()
    for at, source, target in key_pairs:
        own_copies.append(
            pltpu.make_async_copy(
                source.at[:, columns(my_head)], target.at[mine], own_sem.at[at]
            )
        )
        own_copies[-1].start()
    for dz in far_first:
        for dh in range(n_head):
            if (dz, dh) == (0, 0):
                continue
            for at, source, target in key_pairs:
                copy = push(at, source, target, mine, dz, dh)
                copy.start()
                sends.append(copy)
    passes = []
    for at, source, target in key_pairs:
        copy = pltpu.make_async_remote_copy(
            src_ref=source.at[:, columns(my_head)],
            dst_ref=target.at[mine],
            send_sem=pass_send.at[at, my_row],
            recv_sem=pass_recv.at[at, my_row],
            device_id=sibling,
            device_id_type=MESH,
        )
        copy.start()
        passes.append(copy)
    for at, source, target in row_pairs:
        own_copies.append(
            pltpu.make_async_copy(
                source.at[:, columns(my_head)], target.at[my_row], own_sem.at[at]
            )
        )
        own_copies[-1].start()
    for dz in near_first:
        for dh in range(n_head):
            if (dz, dh) == (0, 0):
                continue
            for at, source, target in row_pairs:
                copy = push(at, source, target, my_row, dz, dh)
                copy.start()
                sends.append(copy)

    blank = jnp.zeros((BLOCK, HEAD_DIM), jnp.float32)

    def clear(n, carry):
        k_sum[n] = blank
        v_sum[n] = blank
        return carry

    lax.fori_loop(0, total_blocks, clear, 0)
    none = n_z * runs * PICKS
    k_far[none] = blank.astype(jnp.bfloat16)
    v_far[none] = blank.astype(jnp.bfloat16)

    for dz in [0] + [d for d in far_first if d != 0]:
        for dh in range(n_head):
            if (dz, dh) == (0, 0):
                continue
            z1, h1 = from_peer(dz, dh)
            block = (2 * z1 + c) * runs + h1
            for at, source, target in key_pairs:
                arrival(at, source, target, block, dz, dh).wait_recv()
                copy = pltpu.make_async_remote_copy(
                    src_ref=target.at[block],
                    dst_ref=target.at[block],
                    send_sem=pass_send.at[at, z1 * n_head + h1],
                    recv_sem=pass_recv.at[at, z1 * n_head + h1],
                    device_id=sibling,
                    device_id_type=MESH,
                )
                copy.start()
                passes.append(copy)
    for copy in own_copies:
        copy.wait()
    for row in range(n_z * n_head):
        z1, h1 = row // n_head, row % n_head
        block = (2 * z1 + 1 - c) * runs + h1
        for at, source, target in key_pairs:
            pltpu.make_async_remote_copy(
                src_ref=target.at[block],
                dst_ref=target.at[block],
                send_sem=pass_send.at[at, row],
                recv_sem=pass_recv.at[at, row],
                device_id=sibling,
                device_id_type=MESH,
            ).wait_recv()

    def contract(left, right, dims):
        return lax.dot_general(
            left, right, ((dims[:1], dims[1:]), ((), ())), preferred_element_type=jnp.float32
        )

    def query_step(z1, r):
        row = z1 * runs + r
        block = (2 * z1 + c) * runs + r
        low = (block + total_blocks - 1) % total_blocks
        high = (block + 1) % total_blocks
        picks = [owner_ref[j, block] * runs + r for j in range(PICKS)]
        named = [low, block, high] + picks + [0, 1]
        keys = jnp.concatenate([k_all[n] for n in named], axis=0)
        values = jnp.concatenate([v_all[n] for n in named], axis=0)
        query = q_all[row]
        grad = g_all[row]
        scores = contract(keys, query, (1, 1))
        top = jnp.max(scores, axis=0, keepdims=True)
        weights = jnp.exp((scores - top) * factor)
        weights = weights * (1.0 / jnp.sum(weights, axis=0, keepdims=True))
        rounded = weights.astype(jnp.bfloat16)
        grad_weights = contract(values, grad, (1, 1))
        delta = jnp.sum(weights * grad_weights, axis=0, keepdims=True)
        grad_scores = (weights * (grad_weights - delta) * factor).astype(jnp.bfloat16)
        o_stage[row] = contract(rounded, values, (0, 0)).astype(jnp.bfloat16)
        dq_stage[row] = contract(grad_scores, keys, (0, 0)).astype(jnp.bfloat16)
        key_terms = contract(grad_scores, query, (1, 0))
        value_terms = contract(rounded, grad, (1, 0))
        for j, n in ((0, low), (1, block), (2, high), (6, 0), (7, 1)):
            k_sum[n] += key_terms[j * BLOCK : (j + 1) * BLOCK]
            v_sum[n] += value_terms[j * BLOCK : (j + 1) * BLOCK]
        for j in range(PICKS):
            rows = slice((3 + j) * BLOCK, (4 + j) * BLOCK)
            k_far[row * PICKS + j] = key_terms[rows].astype(jnp.bfloat16)
            v_far[row * PICKS + j] = value_terms[rows].astype(jnp.bfloat16)

    def hand_out(pairs, dz):
        z2 = (z + n_z - dz) % n_z
        for at, stage, out in pairs:
            source = stage.at[pl.ds(z2 * runs, runs)]
            target = out.at[:, :, columns(z)]
            if dz == 0:
                copy = pltpu.make_async_copy(source, target, out_own.at[at])
                copy.start()
                own_outs.append(copy)
            else:
                copy = pltpu.make_async_remote_copy(
                    src_ref=source,
                    dst_ref=target,
                    send_sem=out_send.at[at, z2],
                    recv_sem=out_recv.at[at, z],
                    device_id={"head": head, "blk": 2 * z2 + c},
                    device_id_type=MESH,
                )
                copy.start()
                sends.append(copy)

    own_outs = []
    row_outs = ((0, o_stage, o_out), (1, dq_stage, dq_out))
    key_outs = ((2, dk_stage, dk_out), (3, dv_stage, dv_out))
    for dz in near_first:
        z1 = (z + n_z - dz) % n_z
        for dh in range(n_head):
            if (dz, dh) == (0, 0):
                continue
            h1 = (head + n_head - dh) % n_head
            for at, source, target in row_pairs:
                arrival(at, source, target, z1 * runs + h1, dz, dh).wait_recv()

        def step(r, carry, z1=z1):
            query_step(z1, r)
            return carry

        lax.fori_loop(0, runs, step, 0)
        hand_out(row_outs, dz)

    def total_of(sums, far, run, r):
        total = sums[run * runs + r]
        for z1 in range(n_z):
            block = (2 * z1 + c) * runs + r
            row = z1 * runs + r
            place = none
            for j in range(PICKS):
                place = jnp.where(owner_ref[j, block] == run, row * PICKS + j, place)
            total = total + far[place].astype(jnp.float32)
        return total

    def give_step(row, carry):
        run, r = 2 * (row // runs) + 1 - c, row % runs
        k_give[row] = total_of(k_sum, k_far, run, r).astype(jnp.bfloat16)
        v_give[row] = total_of(v_sum, v_far, run, r).astype(jnp.bfloat16)
        return carry

    lax.fori_loop(0, n_z * runs, give_step, 0)
    pair_copies = []
    for at, give, take in ((0, k_give, k_take), (1, v_give, v_take)):
        copy = pltpu.make_async_remote_copy(
            src_ref=give,
            dst_ref=take,
            send_sem=pair_send.at[at],
            recv_sem=pair_recv.at[at],
            device_id=sibling,
            device_id_type=MESH,
        )
        copy.start()
        pair_copies.append(copy)
    for copy in pair_copies:
        copy.wait_recv()
    for dz in far_first:
        z1 = (z + n_z - dz) % n_z

        def join_step(r, carry, z1=z1):
            row, run = z1 * runs + r, 2 * z1 + c
            for sums, far, take, stage in (
                (k_sum, k_far, k_take, dk_stage),
                (v_sum, v_far, v_take, dv_stage),
            ):
                total = total_of(sums, far, run, r) + take[row].astype(jnp.float32)
                stage[row] = total.astype(jnp.bfloat16)
            return carry

        lax.fori_loop(0, runs, join_step, 0)
        hand_out(key_outs, dz)

    for dz in range(1, n_z):
        z1 = (z + n_z - dz) % n_z
        for at, stage, out in row_outs + key_outs:
            pltpu.make_async_remote_copy(
                src_ref=stage.at[pl.ds(z1 * runs, runs)],
                dst_ref=out.at[:, :, columns(z1)],
                send_sem=out_send.at[at, z1],
                recv_sem=out_recv.at[at, z1],
                device_id=sibling,
                device_id_type=MESH,
            ).wait_recv()
    for copy in own_outs:
        copy.wait()
    for copy in sends + passes + pair_copies:
        copy.wait_send()


def settle_kernel(count, pieces, *refs):
    sources, targets = refs[:count], refs[count : 2 * count]
    held, in_sem, out_sem = refs[2 * count :]
    loads, stores = [], []
    for at in range(count):
        for piece in range(pieces):
            loads.append(
                pltpu.make_async_copy(
                    sources[at].at[piece], held.at[at, piece], in_sem.at[at, piece]
                )
            )
            stores.append(
                pltpu.make_async_copy(
                    held.at[at, piece], targets[at].at[piece], out_sem.at[at, piece]
                )
            )
    for load in loads:
        load.start()
    for load, store in zip(loads, stores):
        load.wait()
        store.start()
    for store in stores:
        store.wait()


def by_heads(queries, keys, values, grad_out, stride_owner):
    n_head, n_blk = lax.axis_size("head"), lax.axis_size("blk")
    n_z = n_blk // 2
    rows = n_z * n_head
    seq_rows, width = BLOCK * n_head, n_z * HEAD_DIM
    tile = (BLOCK, HEAD_DIM)
    low, wide = jnp.bfloat16, jnp.float32
    dma = pltpu.SemaphoreType.DMA
    out = jax.ShapeDtypeStruct((n_head, BLOCK, width), low)
    anywhere = pl.BlockSpec(memory_space=pl.ANY)
    arrived = pl.pallas_call(
        partial(head_kernel, n_head, n_z),
        out_shape=(out,) * 4,
        in_specs=[pl.BlockSpec(memory_space=pltpu.HBM)] * 5,
        out_specs=(anywhere,) * 4,
        scratch_shapes=[
            pltpu.SMEM(stride_owner.shape[::-1], jnp.int32),
            pltpu.VMEM((rows,) + tile, low),
            pltpu.VMEM((2 * rows,) + tile, low),
            pltpu.VMEM((2 * rows,) + tile, low),
            pltpu.VMEM((rows,) + tile, low),
            pltpu.VMEM((2 * rows,) + tile, wide),
            pltpu.VMEM((2 * rows,) + tile, wide),
            pltpu.VMEM((rows * PICKS + 1,) + tile, low),
            pltpu.VMEM((rows * PICKS + 1,) + tile, low),
        ]
        + [pltpu.VMEM((rows,) + tile, low)] * 8
        + [
            dma((4, rows)),
            dma((4, rows)),
            dma((2, rows)),
            dma((2, rows)),
            dma((5,)),
            dma((4, n_z)),
            dma((4, n_z)),
            dma((4,)),
            dma((2,)),
            dma((2,)),
        ],
        compiler_params=pltpu.CompilerParams(
            collective_id=0, has_side_effects=True, vmem_limit_bytes=67043328
        ),
    )(stride_owner.T, queries, keys, values, grad_out)
    settled = pl.pallas_call(
        partial(settle_kernel, 4, n_head),
        out_shape=(out,) * 4,
        in_specs=[pl.BlockSpec(memory_space=pl.ANY)] * 4,
        out_specs=(pl.BlockSpec(memory_space=pl.ANY),) * 4,
        scratch_shapes=[
            pltpu.VMEM((4, n_head, BLOCK, width), low),
            dma((4, n_head)),
            dma((4, n_head)),
        ],
        compiler_params=pltpu.CompilerParams(vmem_limit_bytes=67043328),
    )(*arrived)
    return tuple(part.reshape(seq_rows, width) for part in settled)


def on_device(queries, keys, values, grad_out, stride_owner):
    n_head, n_blk = lax.axis_size("head"), lax.axis_size("blk")
    rows, width = queries.shape
    if rows == BLOCK and n_blk % 2 == 0 and width == n_head * (n_blk // 2) * HEAD_DIM:
        return by_heads(queries, keys, values, grad_out, stride_owner)
    return by_runs(queries, keys, values, grad_out, stride_owner)


def solution(mesh):
    return jax.shard_map(
        on_device,
        mesh=mesh,
        in_specs=(
            P(("blk", "head"), None),
            P(("blk", "head"), None),
            P(("blk", "head"), None),
            P(("blk", "head"), None),
            P(),
        ),
        out_specs=(P("blk", "head"), P("blk", "head"), P("blk", "head"), P("blk", "head")),
        check_vma=False,
    )
```

```python
import math
from functools import partial

import jax
import jax.numpy as jnp
from jax import lax
from jax.experimental import pallas as pl
from jax.experimental.pallas import tpu as pltpu
from jax.sharding import PartitionSpec as P

HEAD_DIM = 128
BLOCK = 128
PICKS = 3
MESH = pl.DeviceIdType.MESH


def with_halo(block, sides, width):
    for axis, dim in sides:
        count = lax.axis_size(axis)
        forward = [(i, i + 1) for i in range(count - 1)]
        forward.append((count - 1, 0))
        backward = [(target, source) for source, target in forward]
        low = lax.ppermute(
            lax.slice_in_dim(block, block.shape[dim] - width, None, axis=dim), axis, forward
        )
        high = lax.ppermute(lax.slice_in_dim(block, 0, width, axis=dim), axis, backward)
        block = jnp.concatenate([low, block, high], axis=dim)
    return block


def from_root(block, axis, holder):
    block = jnp.where(lax.axis_index(axis) == holder, block, jnp.zeros_like(block))
    return lax.psum(block, axis)


def slot_tables(stride_owner, n_blk, blocks, capacity, device):
    owner_table = stride_owner.reshape(n_blk, blocks, PICKS)
    owner_ids = jnp.arange(n_blk, dtype=jnp.int32)
    naming = jnp.any(owner_table[:, :, :, None] == owner_ids[None, None, None, :], axis=2)
    counts = naming.astype(jnp.int32)
    ranking = jnp.cumsum(counts, axis=1) - counts
    naming_here = lax.dynamic_index_in_dim(naming, device, 2, keepdims=False)
    ranking_here = lax.dynamic_index_in_dim(ranking, device, 2, keepdims=False)
    slot_ids = jnp.arange(capacity, dtype=jnp.int32)
    matched = naming_here[:, None, :] & (ranking_here[:, None, :] == slot_ids[None, :, None])
    offsets = jnp.sum(
        matched.astype(jnp.int32) * jnp.arange(blocks, dtype=jnp.int32)[None, None, :], axis=2
    )
    own_rows = lax.dynamic_index_in_dim(owner_table, device, 0, keepdims=False)
    own_ranks = lax.dynamic_index_in_dim(ranking, device, 0, keepdims=False)
    picked = jnp.take_along_axis(own_ranks, own_rows, axis=1)
    flat_slot = own_rows * capacity + picked
    return (offsets.reshape(-1), flat_slot, matched.reshape(n_blk * capacity, blocks))


def fetch_keys(stacked, offsets, flat_slot, capacity):
    seq_rows = stacked.shape[1]
    width = stacked.shape[2]
    blocks = seq_rows // BLOCK
    n_blk = lax.axis_size("blk")
    extended = with_halo(stacked, (("blk", 1),), BLOCK)
    extended = extended.reshape(2, blocks + 2, BLOCK, width)
    block_view = stacked.reshape(2, blocks, BLOCK, width)
    leading = from_root(block_view[:, 0:2], "blk", 0)
    outgoing = jnp.take(block_view, offsets, axis=1).reshape(2, n_blk, capacity, BLOCK, width)
    incoming = lax.all_to_all(outgoing, "blk", split_axis=1, concat_axis=1, tiled=True)
    incoming = incoming.reshape(2, n_blk * capacity, BLOCK, width)
    pooled = jnp.concatenate([extended, incoming, leading], axis=1)
    rows_here = jnp.arange(blocks, dtype=jnp.int32)[:, None]
    nearby_index = rows_here + jnp.arange(3, dtype=jnp.int32)[None, :]
    distant_index = blocks + 2 + flat_slot
    leading_index = (
        jnp.zeros((blocks, 2), jnp.int32)
        + (blocks + 2 + n_blk * capacity)
        + jnp.arange(2, dtype=jnp.int32)[None, :]
    )
    table = jnp.concatenate([nearby_index, distant_index, leading_index], axis=1)
    return jnp.take(pooled, table.reshape(-1), axis=1)


def score_block(query_part, key_part, factor):
    return (
        jnp.einsum("gqhd,gjkhd->ghqjk", query_part, key_part, preferred_element_type=jnp.float32)
        * factor
    )


def log_normal(scores):
    row_max = jnp.max(scores, axis=(3, 4), keepdims=True)
    return row_max + jnp.log(jnp.sum(jnp.exp(scores - row_max), axis=(3, 4), keepdims=True))


def output_of(rounded, value_part):
    return jnp.einsum(
        "ghqjk,gjkhd->gqhd", rounded, value_part, preferred_element_type=jnp.float32
    ).astype(jnp.bfloat16)


def split_terms(coeffs, source):
    group_size = source.shape[0]
    near = jnp.einsum(
        "ghqjk,gqhd->gjkhd", coeffs[:, :, :, 0:3], source, preferred_element_type=jnp.float32
    )
    far = jnp.einsum(
        "ghqjk,gqhd->gjkhd", coeffs[:, :, :, 3:6], source, preferred_element_type=jnp.float32
    ).astype(jnp.bfloat16)
    lead = jnp.einsum(
        "ghqjk,gqhd->jkhd", coeffs[:, :, :, 6:8], source, preferred_element_type=jnp.float32
    )
    near = near.reshape(group_size, 3, near.shape[2], near.shape[3] * near.shape[4])
    far = far.reshape(group_size, 3, far.shape[2], far.shape[3] * far.shape[4])
    lead = lead.reshape(2, lead.shape[1], lead.shape[2] * lead.shape[3])
    return (near, far, lead)


def backward_from(
    scores, log_total, rounded, attended, grad_part, query_part, key_part, value_part, factor
):
    grad_weights = jnp.einsum(
        "gqhd,gjkhd->ghqjk", grad_part, value_part, preferred_element_type=jnp.float32
    )
    delta = jnp.sum(grad_part.astype(jnp.float32) * attended.astype(jnp.float32), axis=3)
    delta = jnp.transpose(delta, (0, 2, 1))[:, :, :, None, None]
    grad_scores = (jnp.exp(scores - log_total) * (grad_weights - delta) * factor).astype(
        jnp.bfloat16
    )
    grad_query = jnp.einsum(
        "ghqjk,gjkhd->gqhd", grad_scores, key_part, preferred_element_type=jnp.float32
    ).astype(jnp.bfloat16)
    key_near, key_far, key_lead = split_terms(grad_scores, query_part)
    value_near, value_far, value_lead = split_terms(rounded, grad_part)
    return (grad_query, key_near, key_far, key_lead, value_near, value_far, value_lead)


def spread_near(near_terms, width):
    blank = jnp.zeros((1, BLOCK, width), jnp.float32)
    return (
        jnp.concatenate([near_terms[:, 0], blank, blank], axis=0)
        + jnp.concatenate([blank, near_terms[:, 1], blank], axis=0)
        + jnp.concatenate([blank, blank, near_terms[:, 2]], axis=0)
    )


def by_runs(queries, keys, values, grad_out, stride_owner):
    query_rows, key_rows, value_rows, grad_rows = (
        lax.all_to_all(queries, "head", split_axis=1, concat_axis=0, tiled=True),
        lax.all_to_all(keys, "head", split_axis=1, concat_axis=0, tiled=True),
        lax.all_to_all(values, "head", split_axis=1, concat_axis=0, tiled=True),
        lax.all_to_all(grad_out, "head", split_axis=1, concat_axis=0, tiled=True),
    )
    seq_rows, width = query_rows.shape
    heads_here = width // HEAD_DIM
    blocks = seq_rows // BLOCK
    n_blk = lax.axis_size("blk")
    capacity = max(2, (PICKS * blocks + n_blk - 1) // n_blk)
    device = lax.axis_index("blk")
    offsets, flat_slot, matched = slot_tables(stride_owner, n_blk, blocks, capacity, device)
    group_size = math.gcd(blocks, max(1, 512 // BLOCK))
    group_count = blocks // group_size
    factor = HEAD_DIM ** (-0.5)
    stacked = jnp.stack([key_rows, value_rows])
    query_view = query_rows.reshape(blocks, BLOCK, heads_here, HEAD_DIM)
    grad_view = grad_rows.reshape(blocks, BLOCK, heads_here, HEAD_DIM)
    key_sets = fetch_keys(stacked, offsets, flat_slot, capacity)
    key_sets = key_sets.reshape(2, blocks, 8, BLOCK, heads_here, HEAD_DIM)

    def pieces(group_id):
        start = group_id * group_size
        query_part = lax.dynamic_slice_in_dim(query_view, start, group_size, 0)
        grad_part = lax.dynamic_slice_in_dim(grad_view, start, group_size, 0)
        kv_part = lax.dynamic_slice_in_dim(key_sets, start, group_size, 1)
        return (query_part, grad_part, kv_part[0], kv_part[1])

    def joined_pass(group_id):
        query_part, grad_part, key_part, value_part = pieces(group_id)
        scores = score_block(query_part, key_part, factor)
        log_total = log_normal(scores)
        rounded = jnp.exp(scores - log_total).astype(jnp.bfloat16)
        attended = output_of(rounded, value_part)
        extra = backward_from(
            scores,
            log_total,
            rounded,
            attended,
            grad_part,
            query_part,
            key_part,
            value_part,
            factor,
        )
        return (attended,) + extra

    group_ids = jnp.arange(group_count, dtype=jnp.int32)
    results = lax.map(joined_pass, group_ids)
    attended = results[0]
    grad_query, key_near, key_far, key_lead, value_near, value_far, value_lead = results[1:]
    key_ext = spread_near(key_near.reshape(blocks, 3, BLOCK, width), width)
    value_ext = spread_near(value_near.reshape(blocks, 3, BLOCK, width), width)
    rim_terms = jnp.stack(
        [
            jnp.stack([key_ext[0], value_ext[0]]),
            jnp.stack([key_ext[blocks + 1], value_ext[blocks + 1]]),
        ]
    )
    beside = with_halo(rim_terms.astype(jnp.bfloat16), (("blk", 0),), 1).astype(rim_terms.dtype)
    key_owned = key_ext[1 : blocks + 1].at[0].add(beside[0, 0]).at[blocks - 1].add(beside[3, 0])
    value_owned = value_ext[1 : blocks + 1].at[0].add(beside[0, 1]).at[blocks - 1].add(beside[3, 1])
    slot_flat = flat_slot.reshape(-1)
    key_back = (
        jnp.zeros((n_blk * capacity, BLOCK, width), jnp.bfloat16)
        .at[slot_flat]
        .set(key_far.reshape(blocks * PICKS, BLOCK, width))
    )
    value_back = (
        jnp.zeros((n_blk * capacity, BLOCK, width), jnp.bfloat16)
        .at[slot_flat]
        .set(value_far.reshape(blocks * PICKS, BLOCK, width))
    )
    key_arrived, value_arrived = (
        lax.all_to_all(
            key_back.reshape(n_blk, capacity, BLOCK, width),
            "blk",
            split_axis=0,
            concat_axis=0,
            tiled=True,
        ),
        lax.all_to_all(
            value_back.reshape(n_blk, capacity, BLOCK, width),
            "blk",
            split_axis=0,
            concat_axis=0,
            tiled=True,
        ),
    )
    match_b = matched.astype(jnp.bfloat16)
    key_owned = key_owned + jnp.einsum(
        "sr,sbc->rbc",
        match_b,
        key_arrived.reshape(n_blk * capacity, BLOCK, width),
        preferred_element_type=jnp.float32,
    )
    value_owned = value_owned + jnp.einsum(
        "sr,sbc->rbc",
        match_b,
        value_arrived.reshape(n_blk * capacity, BLOCK, width),
        preferred_element_type=jnp.float32,
    )
    key_total, value_total = (
        lax.psum(jnp.sum(key_lead, axis=0).astype(jnp.bfloat16), "blk").astype(jnp.float32),
        lax.psum(jnp.sum(value_lead, axis=0).astype(jnp.bfloat16), "blk").astype(jnp.float32),
    )
    at_root = device == 0
    key_owned = key_owned.at[0:2].add(jnp.where(at_root, key_total, jnp.zeros_like(key_total)))
    value_owned = value_owned.at[0:2].add(
        jnp.where(at_root, value_total, jnp.zeros_like(value_total))
    )
    grad_keys = key_owned.astype(jnp.bfloat16).reshape(seq_rows, width)
    grad_values = value_owned.astype(jnp.bfloat16).reshape(seq_rows, width)
    return (
        attended.reshape(seq_rows, width),
        grad_query.reshape(seq_rows, width),
        grad_keys,
        grad_values,
    )


def exchange_barrier(peers):
    barrier = pltpu.get_barrier_semaphore()
    for peer in peers:
        pl.semaphore_signal(barrier, inc=1, device_id=peer, device_id_type=MESH)
    pl.semaphore_wait(barrier, len(peers))


def head_kernel(
    n_head,
    n_z,
    owner_in,
    q_in,
    k_in,
    v_in,
    g_in,
    o_out,
    dq_out,
    dk_out,
    dv_out,
    owner_ref,
    q_all,
    k_all,
    v_all,
    g_all,
    k_sum,
    v_sum,
    k_far,
    v_far,
    o_stage,
    dq_stage,
    dk_stage,
    dv_stage,
    k_give,
    v_give,
    k_take,
    v_take,
    in_send,
    in_recv,
    pass_send,
    pass_recv,
    own_sem,
    out_send,
    out_recv,
    out_own,
    pair_send,
    pair_recv,
):
    head = lax.axis_index("head")
    blk = lax.axis_index("blk")
    z = blk // 2
    c = blk % 2
    runs = n_head
    total_blocks = 2 * n_z * runs
    factor = HEAD_DIM ** (-0.5)
    sibling = {"head": head, "blk": 2 * z + 1 - c}
    offsets = [(dz, dh) for dz in range(n_z) for dh in range(n_head)]
    far_first = [dz for dz in (2, 1, 3, 0) if dz < n_z] + list(range(4, n_z))
    near_first = far_first

    def columns(head_id):
        return pl.ds(pl.multiple_of(head_id * HEAD_DIM, HEAD_DIM), HEAD_DIM)

    def to_peer(dz, dh):
        return (z + dz) % n_z, (head + dh) % n_head

    def from_peer(dz, dh):
        return (z + n_z - dz) % n_z, (head + n_head - dh) % n_head

    peers = []
    for dz, dh in offsets:
        if (dz, dh) != (0, 0):
            z2, h2 = to_peer(dz, dh)
            peers.append({"head": h2, "blk": 2 * z2 + c})
    exchange_barrier(peers + [sibling])

    key_pairs = ((0, k_in, k_all), (1, v_in, v_all))
    row_pairs = ((2, q_in, q_all), (3, g_in, g_all))
    mine = blk * runs + head
    my_row = z * runs + head
    my_head = head * n_z + z

    def push(at, source, target, slot, dz, dh):
        z2, h2 = to_peer(dz, dh)
        return pltpu.make_async_remote_copy(
            src_ref=source.at[:, columns(h2 * n_z + z2)],
            dst_ref=target.at[slot],
            send_sem=in_send.at[at, z2 * n_head + h2],
            recv_sem=in_recv.at[at, my_row],
            device_id={"head": h2, "blk": 2 * z2 + c},
            device_id_type=MESH,
        )

    def arrival(at, source, target, slot, dz, dh):
        z1, h1 = from_peer(dz, dh)
        return pltpu.make_async_remote_copy(
            src_ref=source.at[:, columns(my_head)],
            dst_ref=target.at[slot],
            send_sem=in_send.at[at, z1 * n_head + h1],
            recv_sem=in_recv.at[at, z1 * n_head + h1],
            device_id=sibling,
            device_id_type=MESH,
        )

    sends = []
    own_copies = [pltpu.make_async_copy(owner_in, owner_ref, own_sem.at[4])]
    own_copies[0].start()
    for at, source, target in key_pairs:
        own_copies.append(
            pltpu.make_async_copy(
                source.at[:, columns(my_head)], target.at[mine], own_sem.at[at]
            )
        )
        own_copies[-1].start()
    for dz in far_first:
        for dh in range(n_head):
            if (dz, dh) == (0, 0):
                continue
            for at, source, target in key_pairs:
                copy = push(at, source, target, mine, dz, dh)
                copy.start()
                sends.append(copy)
    passes = []
    for at, source, target in key_pairs:
        copy = pltpu.make_async_remote_copy(
            src_ref=source.at[:, columns(my_head)],
            dst_ref=target.at[mine],
            send_sem=pass_send.at[at, my_row],
            recv_sem=pass_recv.at[at, my_row],
            device_id=sibling,
            device_id_type=MESH,
        )
        copy.start()
        passes.append(copy)
    for at, source, target in row_pairs:
        own_copies.append(
            pltpu.make_async_copy(
                source.at[:, columns(my_head)], target.at[my_row], own_sem.at[at]
            )
        )
        own_copies[-1].start()
    for dz in near_first:
        for dh in range(n_head):
            if (dz, dh) == (0, 0):
                continue
            for at, source, target in row_pairs:
                copy = push(at, source, target, my_row, dz, dh)
                copy.start()
                sends.append(copy)

    blank = jnp.zeros((BLOCK, HEAD_DIM), jnp.float32)

    def clear(n, carry):
        k_sum[n] = blank
        v_sum[n] = blank
        return carry

    lax.fori_loop(0, total_blocks, clear, 0)
    none = n_z * runs * PICKS
    k_far[none] = blank.astype(jnp.bfloat16)
    v_far[none] = blank.astype(jnp.bfloat16)

    for dz in [0] + [d for d in far_first if d != 0]:
        for dh in range(n_head):
            if (dz, dh) == (0, 0):
                continue
            z1, h1 = from_peer(dz, dh)
            block = (2 * z1 + c) * runs + h1
            for at, source, target in key_pairs:
                arrival(at, source, target, block, dz, dh).wait_recv()
                copy = pltpu.make_async_remote_copy(
                    src_ref=target.at[block],
                    dst_ref=target.at[block],
                    send_sem=pass_send.at[at, z1 * n_head + h1],
                    recv_sem=pass_recv.at[at, z1 * n_head + h1],
                    device_id=sibling,
                    device_id_type=MESH,
                )
                copy.start()
                passes.append(copy)
    for copy in own_copies:
        copy.wait()
    for row in range(n_z * n_head):
        z1, h1 = row // n_head, row % n_head
        block = (2 * z1 + 1 - c) * runs + h1
        for at, source, target in key_pairs:
            pltpu.make_async_remote_copy(
                src_ref=target.at[block],
                dst_ref=target.at[block],
                send_sem=pass_send.at[at, row],
                recv_sem=pass_recv.at[at, row],
                device_id=sibling,
                device_id_type=MESH,
            ).wait_recv()

    def contract(left, right, dims):
        return lax.dot_general(
            left, right, ((dims[:1], dims[1:]), ((), ())), preferred_element_type=jnp.float32
        )

    def query_step(z1, r):
        row = z1 * runs + r
        block = (2 * z1 + c) * runs + r
        low = (block + total_blocks - 1) % total_blocks
        high = (block + 1) % total_blocks
        picks = [owner_ref[j, block] * runs + r for j in range(PICKS)]
        named = [low, block, high] + picks + [0, 1]
        keys = jnp.concatenate([k_all[n] for n in named], axis=0)
        values = jnp.concatenate([v_all[n] for n in named], axis=0)
        query = q_all[row]
        grad = g_all[row]
        scores = contract(keys, query, (1, 1))
        top = jnp.max(scores, axis=0, keepdims=True)
        weights = jnp.exp((scores - top) * factor)
        weights = weights * (1.0 / jnp.sum(weights, axis=0, keepdims=True))
        rounded = weights.astype(jnp.bfloat16)
        grad_weights = contract(values, grad, (1, 1))
        delta = jnp.sum(weights * grad_weights, axis=0, keepdims=True)
        grad_scores = (weights * (grad_weights - delta) * factor).astype(jnp.bfloat16)
        o_stage[row] = contract(rounded, values, (0, 0)).astype(jnp.bfloat16)
        dq_stage[row] = contract(grad_scores, keys, (0, 0)).astype(jnp.bfloat16)
        key_terms = contract(grad_scores, query, (1, 0))
        value_terms = contract(rounded, grad, (1, 0))
        for j, n in ((0, low), (1, block), (2, high), (6, 0), (7, 1)):
            k_sum[n] += key_terms[j * BLOCK : (j + 1) * BLOCK]
            v_sum[n] += value_terms[j * BLOCK : (j + 1) * BLOCK]
        for j in range(PICKS):
            rows = slice((3 + j) * BLOCK, (4 + j) * BLOCK)
            k_far[row * PICKS + j] = key_terms[rows].astype(jnp.bfloat16)
            v_far[row * PICKS + j] = value_terms[rows].astype(jnp.bfloat16)

    def hand_out(pairs, dz):
        z2 = (z + n_z - dz) % n_z
        for at, stage, out in pairs:
            source = stage.at[pl.ds(z2 * runs, runs)]
            target = out.at[:, :, columns(z)]
            if dz == 0:
                copy = pltpu.make_async_copy(source, target, out_own.at[at])
                copy.start()
                own_outs.append(copy)
            else:
                copy = pltpu.make_async_remote_copy(
                    src_ref=source,
                    dst_ref=target,
                    send_sem=out_send.at[at, z2],
                    recv_sem=out_recv.at[at, z],
                    device_id={"head": head, "blk": 2 * z2 + c},
                    device_id_type=MESH,
                )
                copy.start()
                sends.append(copy)

    own_outs = []
    row_outs = ((0, o_stage, o_out), (1, dq_stage, dq_out))
    key_outs = ((2, dk_stage, dk_out), (3, dv_stage, dv_out))
    for dz in near_first:
        z1 = (z + n_z - dz) % n_z
        for dh in range(n_head):
            if (dz, dh) == (0, 0):
                continue
            h1 = (head + n_head - dh) % n_head
            for at, source, target in row_pairs:
                arrival(at, source, target, z1 * runs + h1, dz, dh).wait_recv()

        def step(r, carry, z1=z1):
            query_step(z1, r)
            return carry

        lax.fori_loop(0, runs, step, 0)
        hand_out(row_outs, dz)

    def total_of(sums, far, run, r):
        total = sums[run * runs + r]
        for z1 in range(n_z):
            block = (2 * z1 + c) * runs + r
            row = z1 * runs + r
            place = none
            for j in range(PICKS):
                place = jnp.where(owner_ref[j, block] == run, row * PICKS + j, place)
            total = total + far[place].astype(jnp.float32)
        return total

    def give_step(row, carry):
        run, r = 2 * (row // runs) + 1 - c, row % runs
        k_give[row] = total_of(k_sum, k_far, run, r).astype(jnp.bfloat16)
        v_give[row] = total_of(v_sum, v_far, run, r).astype(jnp.bfloat16)
        return carry

    lax.fori_loop(0, n_z * runs, give_step, 0)
    pair_copies = []
    for at, give, take in ((0, k_give, k_take), (1, v_give, v_take)):
        copy = pltpu.make_async_remote_copy(
            src_ref=give,
            dst_ref=take,
            send_sem=pair_send.at[at],
            recv_sem=pair_recv.at[at],
            device_id=sibling,
            device_id_type=MESH,
        )
        copy.start()
        pair_copies.append(copy)
    for copy in pair_copies:
        copy.wait_recv()
    for dz in far_first:
        z1 = (z + n_z - dz) % n_z

        def join_step(r, carry, z1=z1):
            row, run = z1 * runs + r, 2 * z1 + c
            for sums, far, take, stage in (
                (k_sum, k_far, k_take, dk_stage),
                (v_sum, v_far, v_take, dv_stage),
            ):
                total = total_of(sums, far, run, r) + take[row].astype(jnp.float32)
                stage[row] = total.astype(jnp.bfloat16)
            return carry

        lax.fori_loop(0, runs, join_step, 0)
        hand_out(key_outs, dz)

    for dz in range(1, n_z):
        z1 = (z + n_z - dz) % n_z
        for at, stage, out in row_outs + key_outs:
            pltpu.make_async_remote_copy(
                src_ref=stage.at[pl.ds(z1 * runs, runs)],
                dst_ref=out.at[:, :, columns(z1)],
                send_sem=out_send.at[at, z1],
                recv_sem=out_recv.at[at, z1],
                device_id=sibling,
                device_id_type=MESH,
            ).wait_recv()
    for copy in own_outs:
        copy.wait()
    for copy in sends + passes + pair_copies:
        copy.wait_send()


def settle_kernel(count, pieces, *refs):
    sources, targets = refs[:count], refs[count : 2 * count]
    held, in_sem, out_sem = refs[2 * count :]
    loads, stores = [], []
    for at in range(count):
        for piece in range(pieces):
            loads.append(
                pltpu.make_async_copy(
                    sources[at].at[piece], held.at[at, piece], in_sem.at[at, piece]
                )
            )
            stores.append(
                pltpu.make_async_copy(
                    held.at[at, piece], targets[at].at[piece], out_sem.at[at, piece]
                )
            )
    for load in loads:
        load.start()
    for load, store in zip(loads, stores):
        load.wait()
        store.start(priority=1)
    for store in stores:
        store.wait()


def by_heads(queries, keys, values, grad_out, stride_owner):
    n_head, n_blk = lax.axis_size("head"), lax.axis_size("blk")
    n_z = n_blk // 2
    rows = n_z * n_head
    seq_rows, width = BLOCK * n_head, n_z * HEAD_DIM
    tile = (BLOCK, HEAD_DIM)
    low, wide = jnp.bfloat16, jnp.float32
    dma = pltpu.SemaphoreType.DMA
    out = jax.ShapeDtypeStruct((n_head, BLOCK, width), low)
    anywhere = pl.BlockSpec(memory_space=pl.ANY)
    arrived = pl.pallas_call(
        partial(head_kernel, n_head, n_z),
        out_shape=(out,) * 4,
        in_specs=[pl.BlockSpec(memory_space=pltpu.HBM)] * 5,
        out_specs=(anywhere,) * 4,
        scratch_shapes=[
            pltpu.SMEM(stride_owner.shape[::-1], jnp.int32),
            pltpu.VMEM((rows,) + tile, low),
            pltpu.VMEM((2 * rows,) + tile, low),
            pltpu.VMEM((2 * rows,) + tile, low),
            pltpu.VMEM((rows,) + tile, low),
            pltpu.VMEM((2 * rows,) + tile, wide),
            pltpu.VMEM((2 * rows,) + tile, wide),
            pltpu.VMEM((rows * PICKS + 1,) + tile, low),
            pltpu.VMEM((rows * PICKS + 1,) + tile, low),
        ]
        + [pltpu.VMEM((rows,) + tile, low)] * 8
        + [
            dma((4, rows)),
            dma((4, rows)),
            dma((2, rows)),
            dma((2, rows)),
            dma((5,)),
            dma((4, n_z)),
            dma((4, n_z)),
            dma((4,)),
            dma((2,)),
            dma((2,)),
        ],
        compiler_params=pltpu.CompilerParams(
            collective_id=0, has_side_effects=True, vmem_limit_bytes=67043328
        ),
    )(stride_owner.T, queries, keys, values, grad_out)
    settled = pl.pallas_call(
        partial(settle_kernel, 4, n_head),
        out_shape=(out,) * 4,
        in_specs=[pl.BlockSpec(memory_space=pl.ANY)] * 4,
        out_specs=(pl.BlockSpec(memory_space=pl.ANY),) * 4,
        scratch_shapes=[
            pltpu.VMEM((4, n_head, BLOCK, width), low),
            dma((4, n_head)),
            dma((4, n_head)),
        ],
        compiler_params=pltpu.CompilerParams(vmem_limit_bytes=67043328),
    )(*arrived)
    return tuple(part.reshape(seq_rows, width) for part in settled)


def on_device(queries, keys, values, grad_out, stride_owner):
    n_head, n_blk = lax.axis_size("head"), lax.axis_size("blk")
    rows, width = queries.shape
    if rows == BLOCK and n_blk % 2 == 0 and width == n_head * (n_blk // 2) * HEAD_DIM:
        return by_heads(queries, keys, values, grad_out, stride_owner)
    return by_runs(queries, keys, values, grad_out, stride_owner)


def solution(mesh):
    return jax.shard_map(
        on_device,
        mesh=mesh,
        in_specs=(
            P(("blk", "head"), None),
            P(("blk", "head"), None),
            P(("blk", "head"), None),
            P(("blk", "head"), None),
            P(),
        ),
        out_specs=(P("blk", "head"), P("blk", "head"), P("blk", "head"), P("blk", "head")),
        check_vma=False,
    )
```
